32 devices in a mesh: grp: 4 (over z), seq: 8 (over y, x, core).
Axes of the slice: x: 2, y: 2, z: 4, core: 2. Of those that a mesh axis runs over, the one named last changes fastest.
Arguments:
- layer_input: bfloat16 [8, 1536, 2048], P('seq', 'grp'), may hold values from -6 to 6
- cotangent: bfloat16 [8, 1536, 2048], P('seq', 'grp'), may hold values from -6 to 6
- doc_lengths: int32 [8, 4], P('seq'), may hold values from 1 to 768, 1536 in all within a row
- projection_weight: float32 [2048, 1920], P(('grp', 'seq')), may hold values from -0.125 to 0.125
- w_out: float32 [1280, 2048], P(('grp', 'seq')), may hold values from -2.5 to 2.5
- w_gate: float32 [2048, 4608], P(('grp', 'seq')), may hold values from -0.125 to 0.125
- w_up: float32 [2048, 4608], P(('grp', 'seq')), may hold values from -0.125 to 0.125
- w_down: float32 [4608, 2048], P(('grp', 'seq')), may hold values from -0.09375 to 0.09375
- norm_gains: float32 [4224], P(('grp', 'seq')), may hold values from 0.5 to 1.5
- first_moment_projection: float32 [2048, 1920], P(('grp', 'seq')), may hold values from -0.0007324219 to 0.0007324219
- m_out: float32 [1280, 2048], P(('grp', 'seq')), may hold values from -2.670288e-05 to 2.670288e-05
- m_gate: float32 [2048, 4608], P(('grp', 'seq')), may hold values from -0.00015258789 to 0.00015258789
- m_up: float32 [2048, 4608], P(('grp', 'seq')), may hold values from -0.00015258789 to 0.00015258789
- m_down: float32 [4608, 2048], P(('grp', 'seq')), may hold values from -0.00018310547 to 0.00018310547
- m_gains: float32 [4224], P(('grp', 'seq')), may hold values from -0.00061035156 to 0.00061035156
- second_moment_projection: float32 [2048, 1920], P(('grp', 'seq')), may hold values from 1e-08 to 8e-08
- v_out: float32 [1280, 2048], P(('grp', 'seq')), may hold values from 1.3e-11 to 1e-10
- v_gate: float32 [2048, 4608], P(('grp', 'seq')), may hold values from 4e-10 to 3e-09
- v_up: float32 [2048, 4608], P(('grp', 'seq')), may hold values from 4e-10 to 3e-09
- v_down: float32 [4608, 2048], P(('grp', 'seq')), may hold values from 5.5e-10 to 4.4e-09
- v_gains: float32 [4224], P(('grp', 'seq')), may hold values from 8e-09 to 6.4e-08
Outputs:
- output: bfloat16 [8, 1536, 2048], P('seq', 'grp')
- input_grad: float32 [8, 1536, 2048], P('seq', 'grp')
- grad_norm: float32 [], replicated
- new_qkv: float32 [2048, 1920], P(('grp', 'seq'))
- new_out: float32 [1280, 2048], P(('grp', 'seq'))
- new_gate: float32 [2048, 4608], P(('grp', 'seq'))
- new_up: float32 [2048, 4608], P(('grp', 'seq'))
- new_down: float32 [4608, 2048], P(('grp', 'seq'))
- new_gains: float32 [4224], P(('grp', 'seq'))
- new_m_qkv: float32 [2048, 1920], P(('grp', 'seq'))
- new_m_out: float32 [1280, 2048], P(('grp', 'seq'))
- new_m_gate: float32 [2048, 4608], P(('grp', 'seq'))
- new_m_up: float32 [2048, 4608], P(('grp', 'seq'))
- new_m_down: float32 [4608, 2048], P(('grp', 'seq'))
- new_m_gains: float32 [4224], P(('grp', 'seq'))
- new_v_qkv: float32 [2048, 1920], P(('grp', 'seq'))
- new_v_out: float32 [1280, 2048], P(('grp', 'seq'))
- new_v_gate: float32 [2048, 4608], P(('grp', 'seq'))
- new_v_up: float32 [2048, 4608], P(('grp', 'seq'))
- new_v_down: float32 [4608, 2048], P(('grp', 'seq'))
- new_v_gains: float32 [4224], P(('grp', 'seq'))
The draws below stay inside these ranges and needn't reach their ends.
Inputs may be any that keep to these rules, and one draw needn't show every extreme that they name: `doc_lengths`: each row's lengths sum to 1536; in every row the longest document has exactly 768 tokens.
All inputs are finite; a program needn't handle non-finite values.
Results may differ from the reference program's by a relative error of at most 0.012.
The reference program's roundings to bfloat16 on the way count: a program that leaves them out, or rounds other values in their place, can miss the bound.
Values may be sent and summed in bfloat16 or wider, within the bound.
No kernel may reach another device: no remote copies, remote signals or barrier semaphores. Data moves between devices by JAX's collectives and lax.ppermute only.
A program may use at most 384 MiB of HBM per device.

```python
import math
import jax
import jax.numpy as jnp
import numpy as np
from jax import lax

MODEL_DIM = 2048
FF = 4608
QUERY_HEADS = 20
KV_HEAD_COUNT = 5
HEAD_DIM = 64
NDOC = 4
ROW_LENGTH = 1536
ROWS = 8


def block_levels(key, shape, pieces, smallest, top_value):
    def one(axis_at, blocks):
        draws = jax.random.uniform(jax.random.fold_in(jax.random.fold_in(key, 6), axis_at), (blocks,), jnp.float32, smallest / len(pieces), top_value / len(pieces))
        return jnp.repeat(jnp.exp(draws), shape[axis_at] // blocks).reshape((-1,) + (1,) * (len(shape) - axis_at - 1))

    level = one(*pieces[0])
    for cut in pieces[1:]:
        level = level * one(*cut)
    return level


def split_up(count, total, most, lean):
    portions = [(1 << 20) // math.isqrt(rank ** lean) + 1 for rank in range(2, count + 1)]
    surplus, holding = total - most - (count - 1), [1] * (count - 1)
    while surplus > 0:
        free = [i for i in range(count - 1) if holding[i] < most]
        mass, left = sum([portions[i] for i in free]), surplus
        for i in free:
            extra = min(most - holding[i], max(1, left * portions[i] // mass), surplus)
            holding[i] = holding[i] + extra
            surplus = surplus - extra
    return np.array([most] + holding)


def uneven_parts(stream_key, number_of, total, bound, skew):
    if number_of == 2:
        one = jax.random.randint(stream_key, (), max(1, total - bound), min(bound, total - 1) + 1)
        return jnp.stack([one, total - one])
    sizes = jnp.asarray(split_up(number_of, total, bound, skew), jnp.int32)
    twos = (number_of - 1) // 2
    source_of, sink = sizes[1:1 + 2 * twos:2], sizes[2:2 + 2 * twos:2]
    slack = jnp.minimum(source_of - 1, bound - sink)
    moved = jax.random.randint(jax.random.fold_in(stream_key, 1), (twos,), 0, 1 << 20) % (slack + 1)
    sizes = sizes.at[1:1 + 2 * twos:2].set(source_of - moved).at[2:2 + 2 * twos:2].set(sink + moved)
    return sizes[jax.random.permutation(jax.random.fold_in(stream_key, 2), number_of)]


def gaussian(rng, extent, deviation, bound, cuts=(), held_as=jnp.bfloat16):
    entries = deviation * jax.random.normal(rng, extent, jnp.float32)
    if cuts:
        entries = entries * block_levels(rng, extent, cuts, -0.22, 0.18)
    return jnp.clip(entries, -bound, bound).astype(held_as)


def setup_inputs(seed: int = 0) -> dict:
    key_of = jax.random.split(jax.random.key(seed), 22)
    return {
        "layer_input": gaussian(key_of[0], (ROWS, ROW_LENGTH, MODEL_DIM), 1.0, 6.0, ((0, 8), (1, 4))),
        "cotangent": gaussian(key_of[1], (ROWS, ROW_LENGTH, MODEL_DIM), 1.0, 6.0, ((0, 8), (1, 4))),
        "doc_lengths": jax.vmap(lambda own: uneven_parts(own, NDOC, ROW_LENGTH, ROW_LENGTH // 2, 2))(jax.random.split(key_of[2], ROWS)).reshape((ROWS, NDOC)).astype(jnp.int32),
        "projection_weight": gaussian(key_of[3], (MODEL_DIM, QUERY_HEADS * HEAD_DIM + 2 * KV_HEAD_COUNT * HEAD_DIM), MODEL_DIM ** -0.5, 0.125, ((0, 32),), jnp.float32),
        "w_out": gaussian(key_of[4], (QUERY_HEADS * HEAD_DIM, MODEL_DIM), (QUERY_HEADS * HEAD_DIM // 256) ** -0.5, 2.5, ((0, 32),), jnp.float32),
        "w_gate": gaussian(key_of[5], (MODEL_DIM, FF), MODEL_DIM ** -0.5, 0.125, ((0, 32),), jnp.float32),
        "w_up": gaussian(key_of[6], (MODEL_DIM, FF), MODEL_DIM ** -0.5, 0.125, ((0, 32),), jnp.float32),
        "w_down": gaussian(key_of[7], (FF, MODEL_DIM), FF ** -0.5, 0.09375, ((0, 32),), jnp.float32),
        "norm_gains": jnp.clip(1.0 + 0.1 * jax.random.normal(key_of[8], (2 * MODEL_DIM + 2 * HEAD_DIM,), jnp.float32), 0.5, 1.5),
        "first_moment_projection": gaussian(key_of[9], (MODEL_DIM, QUERY_HEADS * HEAD_DIM + 2 * KV_HEAD_COUNT * HEAD_DIM), (4.8e-5), 0.0007324219, ((0, 32),), jnp.float32),
        "m_out": gaussian(key_of[10], (QUERY_HEADS * HEAD_DIM, MODEL_DIM), (1.8e-6), 2.6702880859375e-05, ((0, 32),), jnp.float32),
        "m_gate": gaussian(key_of[11], (MODEL_DIM, FF), (1.0e-5), 0.00015258789, ((0, 32),), jnp.float32),
        "m_up": gaussian(key_of[12], (MODEL_DIM, FF), (1.0e-5), 0.00015258789, ((0, 32),), jnp.float32),
        "m_down": gaussian(key_of[13], (FF, MODEL_DIM), (1.2e-5), 0.00018310547, ((0, 32),), jnp.float32),
        "m_gains": gaussian(key_of[14], (2 * MODEL_DIM + 2 * HEAD_DIM,), (4.4e-5), 0.00061035156, ((0, 32),), jnp.float32),
        "second_moment_projection": jnp.clip(jnp.exp(math.log(7.999999951380232e-08) - 2.0794415 * jax.random.uniform(key_of[15], (MODEL_DIM, QUERY_HEADS * HEAD_DIM + 2 * KV_HEAD_COUNT * HEAD_DIM), jnp.float32) ** block_levels(key_of[15], (MODEL_DIM, QUERY_HEADS * HEAD_DIM + 2 * KV_HEAD_COUNT * HEAD_DIM), ((0, 32),), -0.2, 0.2)), 9.99999993922529e-09, 7.999999951380232e-08),
        "v_out": jnp.clip(jnp.exp(math.log(1.000000013351432e-10) - 2.0402208 * jax.random.uniform(key_of[16], (QUERY_HEADS * HEAD_DIM, MODEL_DIM), jnp.float32) ** block_levels(key_of[16], (QUERY_HEADS * HEAD_DIM, MODEL_DIM), ((0, 32),), -0.2, 0.2)), 1.3000000381735433e-11, 1.000000013351432e-10),
        "v_gate": jnp.clip(jnp.exp(math.log(3.000000026176508e-09) - 2.014903 * jax.random.uniform(key_of[17], (MODEL_DIM, FF), jnp.float32) ** block_levels(key_of[17], (MODEL_DIM, FF), ((0, 32),), -0.2, 0.2)), 4.000000053405728e-10, 3.000000026176508e-09),
        "v_up": jnp.clip(jnp.exp(math.log(3.000000026176508e-09) - 2.014903 * jax.random.uniform(key_of[18], (MODEL_DIM, FF), jnp.float32) ** block_levels(key_of[18], (MODEL_DIM, FF), ((0, 32),), -0.2, 0.2)), 4.000000053405728e-10, 3.000000026176508e-09),
        "v_down": jnp.clip(jnp.exp(math.log(4.3999999199684225e-09) - 2.0794415 * jax.random.uniform(key_of[19], (FF, MODEL_DIM), jnp.float32) ** block_levels(key_of[19], (FF, MODEL_DIM), ((0, 32),), -0.2, 0.2)), 5.499999899960528e-10, 4.3999999199684225e-09),
        "v_gains": jnp.clip(jnp.exp(math.log(6.399999818995639e-08) - 2.0794415 * jax.random.uniform(key_of[20], (2 * MODEL_DIM + 2 * HEAD_DIM,), jnp.float32) ** block_levels(key_of[20], (2 * MODEL_DIM + 2 * HEAD_DIM,), ((0, 32),), -0.2, 0.2)), 7.999999773744548e-09, 6.399999818995639e-08),
    }


eps_norm = 1e-06
beta_one = 0.9
beta_two = 0.95
adam_eps = 1e-08
clip_level = 1.0
step_count = 5
learn_rates = (0.02, 0.4, 0.02, 0.02, 0.015, 0.25)
decay_rates = (0.1, 0.1, 0.1, 0.1, 0.1, 0.0)
highest = lax.Precision.HIGHEST

@jax.custom_vjp
def lower_precision(v):
    return lax.optimization_barrier(v.astype(jnp.bfloat16)).astype(jnp.float32)

@jax.custom_vjp
def lower_backward(v):
    return v

def low_keep(v):
    return (lower_precision(v), None)

def low_pass(kept, grad):
    return (grad,)

def back_keep(v):
    return (v, None)

def back_low(kept, grad):
    return (lower_precision(grad),)
lower_precision.defvjp(low_keep, low_pass)
lower_backward.defvjp(back_keep, back_low)

def matmul_high(left, right):
    return jnp.dot(left, right, precision=highest, preferred_element_type=jnp.float32)

def rms_norm(values, gain_vec):
    return values * lax.rsqrt(lax.optimization_barrier(jnp.mean(values * values, axis=-1, keepdims=True)) + eps_norm) * gain_vec

def rotate(values):
    half_dim = values.shape[-1] // 2
    return jnp.concatenate([-values[..., half_dim:], values[..., :half_dim]], axis=-1)

def rotary(values, cosine, sine_vals):
    return values * cosine[:, None, :] + rotate(values) * sine_vals[:, None, :]

def row_tables(lengths):
    lengths = lengths.astype(jnp.int32)
    ends_at = jnp.cumsum(lengths).astype(jnp.int32)
    starts_at = ends_at - lengths
    positions = jnp.arange(ROW_LENGTH, dtype=jnp.int32)
    document_of_token = lax.optimization_barrier(jnp.sum((positions[:, None] >= ends_at[None, :]).astype(jnp.int32), axis=1)).astype(jnp.int32)
    chosen = document_of_token[:, None] == jnp.arange(NDOC, dtype=jnp.int32)[None, :]
    start_of = lax.optimization_barrier(jnp.sum(jnp.where(chosen, starts_at[None, :], 0), axis=1)).astype(jnp.int32)
    offsets = (positions - start_of).astype(jnp.float32)
    frequency = jnp.exp(jnp.arange(HEAD_DIM // 2, dtype=jnp.float32) * (-2.0 * math.log(10000.0) / HEAD_DIM))
    angles = offsets[:, None] * frequency[None, :]
    cosine = jnp.concatenate([jnp.cos(angles), jnp.cos(angles)], axis=1)
    sine_vals = jnp.concatenate([jnp.sin(angles), jnp.sin(angles)], axis=1)
    return (document_of_token, cosine, sine_vals)

def attend_heads(query_rows, key_input, value_input, document_of_token):
    block_rows = min(512, ROW_LENGTH)
    positions = jnp.arange(ROW_LENGTH, dtype=jnp.int32)

    def one_block(block_index):
        first_row = block_index * block_rows
        rows_q = lax.dynamic_slice_in_dim(query_rows, first_row, block_rows, 0)
        rows_pos = lax.dynamic_slice_in_dim(positions, first_row, block_rows, 0)
        rows_doc = lax.dynamic_slice_in_dim(document_of_token, first_row, block_rows, 0)
        scores = lower_backward(jnp.einsum('bkgd,tkd->kgbt', rows_q, key_input, precision=highest) * 0.125)
        allowed = (rows_doc[:, None] == document_of_token[None, :]) & (positions[None, :] <= rows_pos[:, None])
        scores = jnp.where(allowed[None, None], scores, -1e+30)
        soft_low = lower_precision(jax.nn.softmax(scores, axis=-1))
        return jnp.einsum('kgbt,tkd->bkgd', soft_low, value_input, precision=highest)
    blocks = lax.map(jax.checkpoint(one_block), jnp.arange(ROW_LENGTH // block_rows, dtype=jnp.int32))
    return blocks.reshape(ROW_LENGTH, QUERY_HEADS * HEAD_DIM)

def block_forward(inputs, p_qkv, p_out, p_gate, p_up, p_down, p_gains, document_of_token, cosine, sine_vals):
    gain_attn = p_gains[:MODEL_DIM]
    gain_ffn = p_gains[MODEL_DIM:2 * MODEL_DIM]
    gain_query = p_gains[2 * MODEL_DIM:2 * MODEL_DIM + HEAD_DIM]
    gain_key = p_gains[2 * MODEL_DIM + HEAD_DIM:]
    normed = lower_precision(rms_norm(inputs, gain_attn))
    projection_output = lower_backward(lower_precision(matmul_high(normed, p_qkv)))
    query_rows = projection_output[:, :QUERY_HEADS * HEAD_DIM].reshape(ROW_LENGTH, QUERY_HEADS, HEAD_DIM)
    key_input = projection_output[:, QUERY_HEADS * HEAD_DIM:(QUERY_HEADS + KV_HEAD_COUNT) * HEAD_DIM].reshape(ROW_LENGTH, KV_HEAD_COUNT, HEAD_DIM)
    value_input = projection_output[:, (QUERY_HEADS + KV_HEAD_COUNT) * HEAD_DIM:].reshape(ROW_LENGTH, KV_HEAD_COUNT, HEAD_DIM)
    query_rows = lower_precision(rotary(rms_norm(query_rows, gain_query), cosine, sine_vals))
    key_input = lower_precision(rotary(rms_norm(key_input, gain_key), cosine, sine_vals))
    mixed_output = lower_backward(lower_precision(attend_heads(query_rows.reshape(ROW_LENGTH, KV_HEAD_COUNT, QUERY_HEADS // KV_HEAD_COUNT, HEAD_DIM), key_input, value_input, document_of_token)))
    resid = inputs + lower_backward(matmul_high(mixed_output, p_out))
    normed_ffn = lower_precision(rms_norm(resid, gain_ffn))
    gate_pre = lower_backward(matmul_high(normed_ffn, p_gate))
    up_pre = lower_backward(matmul_high(normed_ffn, p_up))
    hidden = lower_precision(jax.nn.silu(gate_pre) * up_pre)
    return resid + matmul_high(hidden, p_down)

def adam_update(master, first_old, second_old, grad_in, clip_scale, learn_rate, decay_rate):
    clipped = grad_in * clip_scale
    first_new = beta_one * first_old + (1.0 - beta_one) * clipped
    second_new = beta_two * second_old + (1.0 - beta_two) * clipped * clipped
    first_hat = first_new / (1.0 - beta_one ** step_count)
    second_hat = second_new / (1.0 - beta_two ** step_count)
    master_new = master - learn_rate * (first_hat / (jnp.sqrt(second_hat) + adam_eps) + decay_rate * master)
    return (master_new, first_new, second_new)

def reference(layer_input, cotangent, doc_lengths, projection_weight, w_out, w_gate, w_up, w_down, norm_gains, first_moment_projection, m_out, m_gate, m_up, m_down, m_gains, second_moment_projection, v_out, v_gate, v_up, v_down, v_gains):
    masters = (projection_weight, w_out, w_gate, w_up, w_down, norm_gains)
    firsts = (first_moment_projection, m_out, m_gate, m_up, m_down, m_gains)
    seconds = (second_moment_projection, v_out, v_gate, v_up, v_down, v_gains)
    copies = tuple((lower_precision(master) for master in masters))

    def per_row(totals, row_items):
        row_in, row_cot, lengths = row_items
        document_of_token, cosine, sine_vals = row_tables(lengths)

        def apply_layer(inputs, p_qkv, p_out, p_gate, p_up, p_down, p_gains):
            return block_forward(inputs, p_qkv, p_out, p_gate, p_up, p_down, p_gains, document_of_token, cosine, sine_vals)
        result, pullback = jax.vjp(apply_layer, row_in.astype(jnp.float32), copies[0], copies[1], copies[2], copies[3], copies[4], copies[5])
        row_grads = pullback(row_cot.astype(jnp.float32))
        totals = tuple((acc_total + new_grad for acc_total, new_grad in zip(totals, row_grads[1:])))
        return (totals, (result.astype(jnp.bfloat16), row_grads[0]))
    zero_grads = tuple((jnp.zeros(master.shape, jnp.float32) for master in masters))
    totals, outs_rows = lax.scan(per_row, zero_grads, (layer_input, cotangent, doc_lengths))
    output, input_grad = outs_rows
    square_sum = jnp.sum(totals[0] * totals[0])
    for member in range(1, 6):
        square_sum = square_sum + jnp.sum(totals[member] * totals[member])
    grad_norm = jnp.sqrt(square_sum)
    clip_scale = jnp.minimum(1.0, clip_level / (grad_norm + 1e-06))
    results = []
    for member in range(6):
        results.append(adam_update(masters[member], firsts[member], seconds[member], totals[member], clip_scale, learn_rates[member], decay_rates[member]))
    return (output, input_grad, grad_norm, results[0][0], results[1][0], results[2][0], results[3][0], results[4][0], results[5][0], results[0][1], results[1][1], results[2][1], results[3][1], results[4][1], results[5][1], results[0][2], results[1][2], results[2][2], results[3][2], results[4][2], results[5][2])
```

```python
import functools
import math

import jax
import jax.numpy as jnp
import numpy as np
from jax import lax
from jax.experimental import pallas as pl
from jax.experimental.pallas import tpu as pltpu
from jax.sharding import Mesh, PartitionSpec as P

QUERY_HEADS = 20
KV_HEAD_COUNT = 5
HEAD_DIM = 64
GROUP = QUERY_HEADS // KV_HEAD_COUNT

eps_norm = 1e-06
beta_one = 0.9
beta_two = 0.95
adam_eps = 1e-08
clip_level = 1.0
step_count = 5
learn_rates = (0.02, 0.4, 0.02, 0.02, 0.015, 0.25)
decay_rates = (0.1, 0.1, 0.1, 0.1, 0.1, 0.0)

PLANE = ("sy", "sx", "sc")
WIDE = jnp.float32
LOW = jnp.bfloat16


def swap(value, axis):
    return lax.ppermute(value, axis, [(0, 1), (1, 0)])


def shift(value, axis, step):
    size = lax.axis_size(axis)
    return lax.ppermute(value, axis, [(i, (i + step) % size) for i in range(size)])


def after(value, *earlier):
    return lax.optimization_barrier((value,) + earlier)[0]


def butterfly_sum(value):
    for axis in ("sc", "sx", "sy", "grp"):
        size = lax.axis_size(axis)
        bit = 1
        while bit < size:
            value = value + lax.ppermute(value, axis, [(i, i ^ bit) for i in range(size)])
            bit *= 2
    return value


def small_plane():
    return all(lax.axis_size(axis) == 2 for axis in PLANE)


def plane_index():
    return (lax.axis_index("sy") * lax.axis_size("sx") + lax.axis_index("sx")) * 2 + lax.axis_index("sc")


def flip_to(value, axis, name):
    other = jnp.flip(value, axis)
    return jnp.where(lax.axis_index(name) == 1, other, value)


def plane_to_all(chunks):
    count, rows, cols = chunks.shape
    if not small_plane():
        return lax.all_to_all(chunks, PLANE, split_axis=0, concat_axis=0, tiled=True)
    value = chunks.reshape(2, 2, 2, rows, cols)
    for axis, name in enumerate(PLANE):
        value = flip_to(value, axis, name)
    for axis, name in ((2, "sc"), (1, "sx"), (0, "sy")):
        keep = lax.index_in_dim(value, 0, axis, keepdims=True)
        sent = swap(lax.index_in_dim(value, 1, axis, keepdims=True), name)
        value = jnp.concatenate([keep, sent], axis=axis)
    for axis, name in enumerate(PLANE):
        value = flip_to(value, axis, name)
    return value.reshape(count, rows, cols)


def gather_plane(own):
    if not small_plane():
        return list(lax.all_gather(own, PLANE, axis=0))
    half = own.shape[0] // 2
    from_x = swap(own, "sx")
    from_y = swap(own, "sy")
    low = swap(from_x[:half], "sy")
    high = swap(from_y[half:], "sx")
    corner = jnp.concatenate([low, high], axis=0)
    mine = [own, from_x, from_y, corner]
    return mine + [swap(block, "sc") for block in mine]


def scatter_plane(blocks):
    if not small_plane():
        stacked = jnp.stack(blocks, axis=0)
        total = lax.psum_scatter(stacked, PLANE, scatter_dimension=0, tiled=True)
        return total[0].astype(WIDE)
    half = blocks[0].shape[0] // 2
    joined = []
    for k in (3, 1, 2, 0):
        joined.append(blocks[k].astype(WIDE) + swap(blocks[4 + k], "sc").astype(WIDE))
    corner, to_x, to_y, own = joined
    low = swap(corner[:half].astype(LOW), "sy")
    high = swap(corner[half:].astype(LOW), "sx")
    to_x = jnp.concatenate([to_x[:half] + low.astype(WIDE), to_x[half:]], axis=0).astype(LOW)
    to_y = jnp.concatenate([to_y[:half], to_y[half:] + high.astype(WIDE)], axis=0).astype(LOW)
    return own + swap(to_x, "sx").astype(WIDE) + swap(to_y, "sy").astype(WIDE)


def gather_all(shard):
    rows, cols = shard.shape
    if not small_plane():
        return lax.all_gather(shard, ("grp",) + PLANE, axis=0, tiled=True)
    depth = lax.axis_size("grp")
    place = [lax.axis_index(axis) for axis in ("grp", "sy", "sx", "sc")]
    whole = jnp.zeros((depth * 8, rows, cols), shard.dtype)

    def put(whole, piece, dz, dy, dx, dc):
        at = ((((place[0] - dz) % depth) * 2 + (place[1] ^ dy)) * 2 + (place[2] ^ dx)) * 2 + (
            place[3] ^ dc
        )
        return lax.dynamic_update_slice(whole, piece[None], (at, 0, 0))

    held = shard
    for dz in range(depth):
        from_x = swap(held, "sx")
        from_y = swap(held, "sy")
        corner = swap(from_x, "sy") if dz % 2 == 0 else swap(from_y, "sx")
        for dy, dx, piece in ((0, 0, held), (0, 1, from_x), (1, 0, from_y), (1, 1, corner)):
            whole = put(whole, piece, dz, dy, dx, 0)
            whole = put(whole, swap(piece, "sc"), dz, dy, dx, 1)
        if dz + 1 < depth:
            held = shift(held, "grp", 1)
    return whole.reshape(depth * 8 * rows, cols)


def scatter_all(partial):
    if not small_plane():
        return lax.psum_scatter(
            partial, ("grp",) + PLANE, scatter_dimension=0, tiled=True
        ).astype(WIDE)
    depth = lax.axis_size("grp")
    z, y, x, c = [lax.axis_index(axis) for axis in ("grp", "sy", "sx", "sc")]
    cols = partial.shape[1]
    rows = partial.shape[0] // (depth * 8)
    value = partial.reshape(depth, 2, 2, 2, rows, cols)

    def part(v, axis, at):
        return lax.dynamic_index_in_dim(v, at, axis, keepdims=False)

    joined = part(value, 3, c).astype(WIDE) + swap(part(value, 3, 1 - c), "sc").astype(WIDE)
    joined = joined.astype(LOW)
    near, far = part(joined, 1, y), part(joined, 1, 1 - y)
    own, to_x = part(near, 1, x), part(near, 1, 1 - x)
    to_y, corner = part(far, 1, x), part(far, 1, 1 - x)
    half = depth // 2
    low = swap(corner[:half], "sy")
    high = swap(corner[half:], "sx")
    to_x = jnp.concatenate(
        [(to_x[:half].astype(WIDE) + low.astype(WIDE)).astype(LOW), to_x[half:]], axis=0
    )
    to_y = jnp.concatenate(
        [to_y[:half], (to_y[half:].astype(WIDE) + high.astype(WIDE)).astype(LOW)], axis=0
    )
    total = own.astype(WIDE) + swap(to_x, "sx").astype(WIDE) + swap(to_y, "sy").astype(WIDE)
    low_total = total.astype(LOW)
    result = part(total, 0, z)
    for step in range(1, depth):
        result = result + shift(part(low_total, 0, (z + step) % depth), "grp", step).astype(WIDE)
    return result


def rotate(values):
    half = values.shape[-1] // 2
    return jnp.concatenate([-values[:, half:], values[:, :half]], axis=-1)


def unrotate(values):
    half = values.shape[-1] // 2
    return jnp.concatenate([values[:, half:], -values[:, :half]], axis=-1)


def unit_of(raw):
    values = raw.astype(WIDE)
    inverse = lax.rsqrt(jnp.mean(values * values, axis=-1, keepdims=True) + eps_norm)
    return values * inverse, inverse


def turned(unit, gain, cos, sin):
    gained = unit * gain
    return (gained * cos + rotate(gained) * sin).astype(LOW)


def norm_back(grad_out, unit_vals, inv_rms, gain_vec):
    scaled = grad_out * gain_vec
    return inv_rms * (scaled - unit_vals * jnp.mean(scaled * unit_vals, axis=-1, keepdims=True))


NT = (((1,), (1,)), ((), ()))
TN = (((0,), (0,)), ((), ()))


def fill_bias(bias_ref, doc_q_ref, doc_k_ref):
    rows, window = bias_ref.shape
    row_at = lax.broadcasted_iota(jnp.int32, (rows, window), 0) + (window - rows)
    col_at = lax.broadcasted_iota(jnp.int32, (rows, window), 1)
    allowed = (doc_q_ref[...] == doc_k_ref[...]) & (col_at <= row_at)
    bias_ref[...] = jnp.where(allowed, 0.0, -1e30).astype(WIDE)


def attend_kernel(q_ref, kv_ref, cos_ref, sin_ref, gain_ref, doc_q_ref, doc_k_ref, o_ref, lse_ref, bias_ref):
    rows, window = bias_ref.shape

    @pl.when(pl.program_id(0) == 0)
    def _():
        fill_bias(bias_ref, doc_q_ref, doc_k_ref)

    gain_q, gain_k = gain_ref[0:1, :], gain_ref[1:2, :]
    cos_q, sin_q = cos_ref[window - rows :, :], sin_ref[window - rows :, :]
    k_unit, _ = unit_of(kv_ref[:, :HEAD_DIM])
    k_low = turned(k_unit, gain_k, cos_ref[...], sin_ref[...])
    v_low = kv_ref[:, HEAD_DIM:]
    for head in range(GROUP):
        cols = slice(head * HEAD_DIM, (head + 1) * HEAD_DIM)
        q_unit, _ = unit_of(q_ref[:, cols])
        q_low = turned(q_unit, gain_q, cos_q, sin_q) * 0.125
        scores = lax.dot_general(q_low, k_low, NT, preferred_element_type=WIDE) + bias_ref[...]
        peak = jnp.max(scores, axis=-1, keepdims=True)
        weights = jnp.exp(scores - peak)
        total = jnp.sum(weights, axis=-1, keepdims=True)
        soft_low = (weights * (1.0 / total)).astype(LOW)
        o_ref[:, cols] = jnp.dot(soft_low, v_low, preferred_element_type=WIDE).astype(LOW)
        lse_ref[0, :, head : head + 1] = peak + jnp.log(total)


def attend(q, kv, cos, sin, gain, doc_q, doc_k):
    rows, window = q.shape[0], kv.shape[0]
    fixed = lambda g: (0, 0)
    return pl.pallas_call(
        attend_kernel,
        grid=(KV_HEAD_COUNT,),
        in_specs=[
            pl.BlockSpec((rows, GROUP * HEAD_DIM), lambda g: (0, g)),
            pl.BlockSpec((window, 2 * HEAD_DIM), lambda g: (0, g)),
            pl.BlockSpec((window, HEAD_DIM), fixed),
            pl.BlockSpec((window, HEAD_DIM), fixed),
            pl.BlockSpec((2, HEAD_DIM), fixed),
            pl.BlockSpec((rows, 1), fixed),
            pl.BlockSpec((1, window), fixed),
        ],
        out_specs=[
            pl.BlockSpec((rows, GROUP * HEAD_DIM), lambda g: (0, g)),
            pl.BlockSpec((1, rows, GROUP), lambda g: (g, 0, 0)),
        ],
        out_shape=[
            jax.ShapeDtypeStruct((rows, QUERY_HEADS * HEAD_DIM), LOW),
            jax.ShapeDtypeStruct((KV_HEAD_COUNT, rows, GROUP), WIDE),
        ],
        scratch_shapes=[pltpu.VMEM((rows, window), WIDE)],
        cost_estimate=pl.CostEstimate(
            flops=4 * rows * window * HEAD_DIM * QUERY_HEADS * 4,
            transcendentals=rows * window * QUERY_HEADS,
            bytes_accessed=rows * 1280 * 4 + window * 1280,
        ),
        name="attend",
    )(q, kv, cos, sin, gain, doc_q, doc_k)


def attend_back_kernel(
    q_ref, kv_ref, cos_ref, sin_ref, gain_ref, doc_q_ref, doc_k_ref, lse_ref, dm_ref,
    dq_ref, dkv_ref, dgain_ref, bias_ref,
):
    rows, window = bias_ref.shape

    @pl.when(pl.program_id(0) == 0)
    def _():
        fill_bias(bias_ref, doc_q_ref, doc_k_ref)
        dgain_ref[...] = jnp.zeros_like(dgain_ref)

    gain_q, gain_k = gain_ref[0:1, :], gain_ref[1:2, :]
    cos_q, sin_q = cos_ref[window - rows :, :], sin_ref[window - rows :, :]
    k_unit, k_inv = unit_of(kv_ref[:, :HEAD_DIM])
    k_low = turned(k_unit, gain_k, cos_ref[...], sin_ref[...])
    v_low = kv_ref[:, HEAD_DIM:]
    dk = jnp.zeros((window, HEAD_DIM), WIDE)
    dv = jnp.zeros((window, HEAD_DIM), WIDE)
    gain_sum = jnp.zeros((1, HEAD_DIM), WIDE)
    for head in range(GROUP):
        cols = slice(head * HEAD_DIM, (head + 1) * HEAD_DIM)
        q_unit, q_inv = unit_of(q_ref[:, cols])
        q_low = turned(q_unit, gain_q, cos_q, sin_q) * 0.125
        grad = dm_ref[:, cols]
        scores = lax.dot_general(q_low, k_low, NT, preferred_element_type=WIDE) + bias_ref[...]
        soft = jnp.exp(scores - lse_ref[0, :, head : head + 1])
        d_soft = lax.dot_general(grad, v_low, NT, preferred_element_type=WIDE)
        delta = jnp.sum(soft * d_soft, axis=-1, keepdims=True)
        d_score = (soft * (d_soft - delta)).astype(LOW)
        dq_hat = jnp.dot(d_score, k_low, preferred_element_type=WIDE) * 0.125
        dk = dk + lax.dot_general(d_score, q_low, TN, preferred_element_type=WIDE)
        dv = dv + lax.dot_general(soft.astype(LOW), grad, TN, preferred_element_type=WIDE)
        dq_gained = dq_hat * cos_q + unrotate(dq_hat * sin_q)
        gain_sum = gain_sum + jnp.sum(dq_gained * q_unit, axis=0, keepdims=True)
        dq_ref[:, cols] = norm_back(dq_gained, q_unit, q_inv, gain_q).astype(LOW)
    dk_gained = dk * cos_ref[...] + unrotate(dk * sin_ref[...])
    dgain_ref[0:1, :] = dgain_ref[0:1, :] + gain_sum
    dgain_ref[1:2, :] = dgain_ref[1:2, :] + jnp.sum(dk_gained * k_unit, axis=0, keepdims=True)
    dkv_ref[:, :HEAD_DIM] = norm_back(dk_gained, k_unit, k_inv, gain_k)
    dkv_ref[:, HEAD_DIM:] = dv


def attend_back(q, kv, cos, sin, gain, doc_q, doc_k, lse, d_mix):
    rows, window = q.shape[0], kv.shape[0]
    fixed = lambda g: (0, 0)
    wide_block = pl.BlockSpec((rows, GROUP * HEAD_DIM), lambda g: (0, g))
    pair_block = pl.BlockSpec((window, 2 * HEAD_DIM), lambda g: (0, g))
    return pl.pallas_call(
        attend_back_kernel,
        grid=(KV_HEAD_COUNT,),
        in_specs=[
            wide_block,
            pair_block,
            pl.BlockSpec((window, HEAD_DIM), fixed),
            pl.BlockSpec((window, HEAD_DIM), fixed),
            pl.BlockSpec((2, HEAD_DIM), fixed),
            pl.BlockSpec((rows, 1), fixed),
            pl.BlockSpec((1, window), fixed),
            pl.BlockSpec((1, rows, GROUP), lambda g: (g, 0, 0)),
            wide_block,
        ],
        out_specs=[wide_block, pair_block, pl.BlockSpec((2, HEAD_DIM), fixed)],
        out_shape=[
            jax.ShapeDtypeStruct((rows, QUERY_HEADS * HEAD_DIM), LOW),
            jax.ShapeDtypeStruct((window, KV_HEAD_COUNT * 2 * HEAD_DIM), WIDE),
            jax.ShapeDtypeStruct((2, HEAD_DIM), WIDE),
        ],
        scratch_shapes=[pltpu.VMEM((rows, window), WIDE)],
        cost_estimate=pl.CostEstimate(
            flops=10 * rows * window * HEAD_DIM * QUERY_HEADS * 4,
            transcendentals=rows * window * QUERY_HEADS,
            bytes_accessed=rows * 1280 * 6 + window * 640 * 6,
        ),
        name="attend_back",
    )(q, kv, cos, sin, gain, doc_q, doc_k, lse, d_mix)


def feed_kernel(main, nf_ref, c_ref, wgu_ref, wd_ref, hid_ref, dgu_ref, out_ref, dnf_ref):
    width = wd_ref.shape[0]
    rest = width - main
    both = jnp.dot(nf_ref[...], wgu_ref[...], preferred_element_type=WIDE)
    d_hidden = lax.dot_general(c_ref[...], wd_ref[...], NT, preferred_element_type=WIDE)

    def one(gate, up, d_hid, hid_at, gate_at, up_at, size):
        sig = jax.nn.sigmoid(gate)
        silu = gate * sig
        hid_ref[:, hid_at : hid_at + size] = (silu * up).astype(LOW)
        dgu_ref[:, gate_at : gate_at + size] = (
            d_hid * up * (sig * (1.0 + gate * (1.0 - sig)))
        ).astype(LOW)
        dgu_ref[:, up_at : up_at + size] = (d_hid * silu).astype(LOW)

    one(both[:, :main], both[:, main : 2 * main], d_hidden[:, :main], 0, 0, main, main)
    if rest:
        one(
            both[:, 2 * main : 2 * main + rest],
            both[:, 2 * main + rest :],
            d_hidden[:, main:],
            main,
            2 * main,
            2 * main + rest,
            rest,
        )
    out_ref[...] = jnp.dot(hid_ref[...], wd_ref[...], preferred_element_type=WIDE).astype(LOW)
    dnf_ref[...] = lax.dot_general(
        dgu_ref[...], wgu_ref[...], NT, preferred_element_type=WIDE
    ).astype(LOW)


def feed(nf, c, wgu, wd, tile):
    tokens, model = nf.shape
    width = wd.shape[0]
    main = width // 128 * 128
    fixed = lambda t: (0, 0)
    by_token = lambda t: (t, 0)
    return pl.pallas_call(
        functools.partial(feed_kernel, main),
        grid=(tokens // tile,),
        in_specs=[
            pl.BlockSpec((tile, model), by_token),
            pl.BlockSpec((tile, model), by_token),
            pl.BlockSpec((model, 2 * width), fixed),
            pl.BlockSpec((width, model), fixed),
        ],
        out_specs=[
            pl.BlockSpec((tile, width), by_token),
            pl.BlockSpec((tile, 2 * width), by_token),
            pl.BlockSpec((tile, model), by_token),
            pl.BlockSpec((tile, model), by_token),
        ],
        out_shape=[
            jax.ShapeDtypeStruct((tokens, width), LOW),
            jax.ShapeDtypeStruct((tokens, 2 * width), LOW),
            jax.ShapeDtypeStruct((tokens, model), LOW),
            jax.ShapeDtypeStruct((tokens, model), LOW),
        ],
        cost_estimate=pl.CostEstimate(
            flops=2 * tokens * model * width * 6,
            transcendentals=tokens * width,
            bytes_accessed=tokens * model * 8 + model * width * 6,
        ),
        name="feed",
    )(nf, c, wgu, wd)


def row_tables(lengths, positions):
    doc_count = lengths.shape[0]
    ends_at = jnp.cumsum(lengths)
    starts_at = ends_at - lengths
    document = jnp.sum((positions[:, None] >= ends_at[None, :]).astype(jnp.int32), axis=1)
    chosen = document[:, None] == jnp.arange(doc_count, dtype=jnp.int32)[None, :]
    start_of = jnp.sum(jnp.where(chosen, starts_at[None, :], 0), axis=1)
    offsets = (positions - start_of).astype(WIDE)
    frequency = jnp.exp(
        jnp.arange(HEAD_DIM // 2, dtype=WIDE) * (-2.0 * math.log(10000.0) / HEAD_DIM)
    )
    angles = offsets[:, None] * frequency[None, :]
    cosine = jnp.cos(angles)
    sine = jnp.sin(angles)
    return (
        document,
        jnp.concatenate([cosine, cosine], axis=1),
        jnp.concatenate([sine, sine], axis=1),
    )


def adam_update(master, first_old, second_old, grad_in, clip_scale, learn_rate, decay_rate):
    clipped = grad_in * clip_scale
    first_new = beta_one * first_old + (1.0 - beta_one) * clipped
    second_new = beta_two * second_old + (1.0 - beta_two) * clipped * clipped
    first_hat = first_new / (1.0 - beta_one**step_count)
    second_hat = second_new / (1.0 - beta_two**step_count)
    master_new = master - learn_rate * (
        first_hat / (jnp.sqrt(second_hat) + adam_eps) + decay_rate * master
    )
    return (master_new, first_new, second_new)


def pair_columns(weight):
    rows = weight.shape[0]
    q_cols = QUERY_HEADS * HEAD_DIM
    pairs = weight[:, q_cols:].reshape(rows, 2, KV_HEAD_COUNT, HEAD_DIM)
    return jnp.concatenate(
        [weight[:, :q_cols], pairs.transpose(0, 2, 1, 3).reshape(rows, -1)], axis=1
    )


def unpair_columns(weight):
    rows = weight.shape[0]
    q_cols = QUERY_HEADS * HEAD_DIM
    pairs = weight[:, q_cols:].reshape(rows, KV_HEAD_COUNT, 2, HEAD_DIM)
    return jnp.concatenate(
        [weight[:, :q_cols], pairs.transpose(0, 2, 1, 3).reshape(rows, -1)], axis=1
    )


def to_slices(weight, depth, plane):
    rows, ff = weight.shape
    return (
        weight.reshape(rows, depth, plane, ff // (depth * plane))
        .transpose(2, 0, 1, 3)
        .reshape(plane, rows, ff // plane)
    )


def from_slices(slices, depth):
    plane, rows, width = slices.shape
    return (
        slices.reshape(plane, rows, depth, width // depth)
        .transpose(1, 2, 0, 3)
        .reshape(rows, plane * width)
    )


def local(
    layer_input, cotangent, doc_lengths,
    projection_weight, w_out, w_gate, w_up, w_down, norm_gains,
    first_moment_projection, m_out, m_gate, m_up, m_down, m_gains,
    second_moment_projection, v_out, v_gate, v_up, v_down, v_gains,
):
    depth = lax.axis_size("grp")
    plane = lax.axis_size("sy") * lax.axis_size("sx") * lax.axis_size("sc")
    z = lax.axis_index("grp")
    member = plane_index()
    tokens, model = layer_input.shape[1], layer_input.shape[2]
    seq_length = depth * tokens
    longest = seq_length // 2
    back_blocks = min(depth - 1, -(-(longest - 1) // tokens))
    window = (back_blocks + 1) * tokens
    q_cols = QUERY_HEADS * HEAD_DIM

    device = z * plane + member
    gain_rows = jnp.zeros((depth * plane, norm_gains.shape[0]), WIDE)
    gain_rows = lax.dynamic_update_slice(
        gain_rows, norm_gains.astype(LOW).astype(WIDE)[None], (device, 0)
    )
    gains = butterfly_sum(gain_rows).reshape(-1)
    gain_attn = gains[:model]
    gain_ffn = gains[model : 2 * model]
    gain_heads = gains[2 * model :].reshape(2, HEAD_DIM)

    qkv_weight = gather_all(pair_columns(projection_weight.astype(LOW)))
    down_weight = lax.all_gather(w_down.astype(LOW), "grp", axis=0, tiled=True)
    width = down_weight.shape[0]
    main = width // 128 * 128
    gate_cut = to_slices(w_gate.astype(LOW), depth, plane)
    up_cut = to_slices(w_up.astype(LOW), depth, plane)
    cut = jnp.concatenate(
        [gate_cut[..., :main], up_cut[..., :main], gate_cut[..., main:], up_cut[..., main:]], axis=-1
    )
    cut = plane_to_all(cut).reshape(-1, 2 * width)
    both_weight = lax.all_gather(cut, "grp", axis=0, tiled=True)
    out_weight = gather_all(w_out.astype(LOW))
    grad_out = cotangent[0]
    grad_blocks = gather_plane(grad_out)

    positions = (z - back_blocks) * tokens + jnp.arange(window, dtype=jnp.int32)
    document, cosine, sine = row_tables(doc_lengths[0], positions)
    doc_k = jnp.where(positions >= 0, document, -1)[None, :]
    doc_q = document[window - tokens :, None]
    inputs = layer_input[0].astype(WIDE)
    inv_attn = lax.rsqrt(jnp.mean(inputs * inputs, axis=-1, keepdims=True) + eps_norm)
    unit_attn = inputs * inv_attn
    normed = (unit_attn * gain_attn).astype(LOW)
    pair_own = jnp.dot(normed, qkv_weight[:, q_cols:], preferred_element_type=WIDE).astype(LOW)
    query = jnp.dot(normed, qkv_weight[:, :q_cols], preferred_element_type=WIDE).astype(LOW)
    pairs = [pair_own]
    onward = [(i, i + 1) for i in range(depth - 1)]
    backward = [(i + 1, i) for i in range(depth - 1)]
    for _ in range(back_blocks):
        pairs.append(lax.ppermute(pairs[-1], "grp", onward))
    pair_all = jnp.concatenate(pairs[::-1], axis=0)
    mix, lse = attend(query, pair_all, cosine, sine, gain_heads, doc_q, doc_k)
    resid = inputs + jnp.dot(mix, out_weight, preferred_element_type=WIDE)
    inv_ffn = lax.rsqrt(jnp.mean(resid * resid, axis=-1, keepdims=True) + eps_norm)
    unit_ffn = resid * inv_ffn
    normed_ffn = (unit_ffn * gain_ffn).astype(LOW)

    nf_all = jnp.concatenate(gather_plane(normed_ffn), axis=0)
    c_all = jnp.concatenate(grad_blocks, axis=0)
    hidden, d_both, out_part, nf_part = feed(nf_all, c_all, both_weight, down_weight, tokens)
    split = lambda value: [value[i * tokens : (i + 1) * tokens] for i in range(plane)]
    d_norm_ffn = scatter_plane(split(nf_part))
    both_grad = lax.dot_general(nf_all, d_both, TN, preferred_element_type=WIDE).astype(LOW)
    both_sum = lax.psum_scatter(both_grad, "grp", scatter_dimension=0, tiled=True)
    down_grad = lax.dot_general(hidden, c_all, TN, preferred_element_type=WIDE).astype(LOW)
    down_sum = lax.psum_scatter(down_grad, "grp", scatter_dimension=0, tiled=True).astype(WIDE)
    output = (resid + scatter_plane(split(out_part))).astype(LOW)

    gain_ffn_grad = jnp.sum(d_norm_ffn * unit_ffn, axis=0)
    d_resid = grad_out.astype(WIDE) + norm_back(d_norm_ffn, unit_ffn, inv_ffn, gain_ffn)
    d_attn = d_resid.astype(LOW)
    d_mix = lax.dot_general(d_attn, out_weight, NT, preferred_element_type=WIDE).astype(LOW)
    out_grad = lax.dot_general(mix, d_attn, TN, preferred_element_type=WIDE).astype(LOW)

    d_query, d_pairs, head_gain_grad = attend_back(
        query, pair_all, cosine, sine, gain_heads, doc_q, doc_k, lse, d_mix
    )
    moving = None
    for block in range(back_blocks):
        part = d_pairs[block * tokens : (block + 1) * tokens]
        if moving is not None:
            part = part + moving.astype(WIDE)
        moving = lax.ppermute(part.astype(LOW), "grp", backward)
    d_pair = d_pairs[window - tokens :]
    if moving is not None:
        d_pair = d_pair + moving.astype(WIDE)
    d_qkv = jnp.concatenate([d_query, d_pair.astype(LOW)], axis=1)
    qkv_grad = lax.dot_general(normed, d_qkv, TN, preferred_element_type=WIDE).astype(LOW)
    d_normed = lax.dot_general(d_qkv, qkv_weight, NT, preferred_element_type=WIDE)
    gain_attn_grad = jnp.sum(d_normed * unit_attn, axis=0)
    input_grad = d_resid + norm_back(d_normed, unit_attn, inv_attn, gain_attn)

    out_sum = scatter_all(out_grad)
    slices = plane_to_all(both_sum.reshape(plane, -1, 2 * width)).astype(WIDE)
    rest = width - main
    gate_slices = jnp.concatenate([slices[..., :main], slices[..., 2 * main : 2 * main + rest]], axis=-1)
    up_slices = jnp.concatenate([slices[..., main : 2 * main], slices[..., 2 * main + rest :]], axis=-1)
    gate_sum = from_slices(gate_slices, depth)
    up_sum = from_slices(up_slices, depth)
    qkv_sum = unpair_columns(scatter_all(qkv_grad))
    shards = [qkv_sum, out_sum, gate_sum, up_sum, down_sum]
    local_square = jnp.sum(shards[0] * shards[0])
    for shard in shards[1:]:
        local_square = local_square + jnp.sum(shard * shard)
    gain_grad = jnp.concatenate([gain_attn_grad, gain_ffn_grad, head_gain_grad.reshape(-1)])
    gain_count = gain_grad.shape[0]
    packed = jnp.concatenate([gain_grad, jnp.full((128,), local_square, WIDE)]).reshape(-1, 128)
    packed = butterfly_sum(packed).reshape(-1)
    gain_total = packed[:gain_count]
    grad_norm = jnp.sqrt(packed[gain_count] + jnp.sum(gain_total * gain_total))
    clip_scale = jnp.minimum(1.0, clip_level / (grad_norm + 1e-06))
    own_gains = norm_gains.shape[0]
    shards.append(lax.dynamic_slice(gain_total, (device * own_gains,), (own_gains,)))

    masters = (projection_weight, w_out, w_gate, w_up, w_down, norm_gains)
    firsts = (first_moment_projection, m_out, m_gate, m_up, m_down, m_gains)
    seconds = (second_moment_projection, v_out, v_gate, v_up, v_down, v_gains)
    results = [
        adam_update(w, m, v, g, clip_scale, lr, wd)
        for w, m, v, g, lr, wd in zip(masters, firsts, seconds, shards, learn_rates, decay_rates)
    ]
    return (
        output[None],
        input_grad[None],
        grad_norm,
        *[r[0] for r in results],
        *[r[1] for r in results],
        *[r[2] for r in results],
    )


def solution(mesh):
    depth, plane = mesh.shape["grp"], mesh.shape["seq"]
    side = math.isqrt(plane // 2)
    inner = Mesh(
        np.asarray(mesh.devices).reshape(depth, plane // 2 // side, side, 2),
        ("grp",) + PLANE,
    )
    rows = P(("grp",) + PLANE, None)
    vector = P(("grp",) + PLANE)
    block = P(PLANE, "grp", None)
    params = (rows,) * 5 + (vector,)
    return jax.shard_map(
        local,
        mesh=inner,
        in_specs=(block, block, P(PLANE, None)) + params * 3,
        out_specs=(block, block, P()) + params * 3,
        check_vma=False,
    )
```

```python
import functools
import math

import jax
import jax.numpy as jnp
import numpy as np
from jax import lax
from jax.experimental import pallas as pl
from jax.experimental.pallas import tpu as pltpu
from jax.sharding import Mesh, PartitionSpec as P

QUERY_HEADS = 20
KV_HEAD_COUNT = 5
HEAD_DIM = 64
GROUP = QUERY_HEADS // KV_HEAD_COUNT

eps_norm = 1e-06
beta_one = 0.9
beta_two = 0.95
adam_eps = 1e-08
clip_level = 1.0
step_count = 5
learn_rates = (0.02, 0.4, 0.02, 0.02, 0.015, 0.25)
decay_rates = (0.1, 0.1, 0.1, 0.1, 0.1, 0.0)

PLANE = ("sy", "sx", "sc")
WIDE = jnp.float32
LOW = jnp.bfloat16


def swap(value, axis):
    return lax.ppermute(value, axis, [(0, 1), (1, 0)])


def shift(value, axis, step):
    size = lax.axis_size(axis)
    return lax.ppermute(value, axis, [(i, (i + step) % size) for i in range(size)])


def after(value, *earlier):
    return lax.optimization_barrier((value,) + earlier)[0]


def butterfly_sum(value):
    for axis in ("sc", "sx", "sy", "grp"):
        size = lax.axis_size(axis)
        bit = 1
        while bit < size:
            value = value + lax.ppermute(value, axis, [(i, i ^ bit) for i in range(size)])
            bit *= 2
    return value


def small_plane():
    return all(lax.axis_size(axis) == 2 for axis in PLANE)


def plane_index():
    return (lax.axis_index("sy") * lax.axis_size("sx") + lax.axis_index("sx")) * 2 + lax.axis_index("sc")


def pick(value, axis, at):
    return lax.dynamic_index_in_dim(value, at, axis, keepdims=False)


def flip_to(value, axis, name):
    other = jnp.flip(value, axis)
    return jnp.where(lax.axis_index(name) == 1, other, value)


def plane_to_all(chunks):
    count, rows, cols = chunks.shape
    if not small_plane():
        return lax.all_to_all(chunks, PLANE, split_axis=0, concat_axis=0, tiled=True)
    value = chunks.reshape(2, 2, 2, rows, cols)
    for axis, name in enumerate(PLANE):
        value = flip_to(value, axis, name)
    for axis, name in ((2, "sc"), (1, "sx"), (0, "sy")):
        keep = lax.index_in_dim(value, 0, axis, keepdims=True)
        sent = swap(lax.index_in_dim(value, 1, axis, keepdims=True), name)
        value = jnp.concatenate([keep, sent], axis=axis)
    for axis, name in enumerate(PLANE):
        value = flip_to(value, axis, name)
    return value.reshape(count, rows, cols)


def gather_plane(own):
    if not small_plane():
        return list(lax.all_gather(own, PLANE, axis=0))
    half = own.shape[0] // 2
    from_x = swap(own, "sx")
    from_y = swap(own, "sy")
    low = swap(from_x[:half], "sy")
    high = swap(from_y[half:], "sx")
    corner = jnp.concatenate([low, high], axis=0)
    mine = [own, from_x, from_y, corner]
    return mine + [swap(block, "sc") for block in mine]


def scatter_begin(blocks):
    if not small_plane():
        return blocks
    half = blocks[0].shape[0] // 2
    joined = []
    for k in (3, 1, 2, 0):
        joined.append(blocks[k].astype(WIDE) + swap(blocks[4 + k], "sc").astype(WIDE))
    corner, to_x, to_y, own = joined
    low = swap(corner[:half].astype(LOW), "sy")
    high = swap(corner[half:].astype(LOW), "sx")
    to_x = jnp.concatenate([to_x[:half] + low.astype(WIDE), to_x[half:]], axis=0).astype(LOW)
    to_y = jnp.concatenate([to_y[:half], to_y[half:] + high.astype(WIDE)], axis=0).astype(LOW)
    return own, to_x, to_y


def scatter_send(begun):
    if not small_plane():
        return begun
    own, to_x, to_y = begun
    return own, swap(to_x, "sx"), swap(to_y, "sy")


def scatter_end(begun):
    if not small_plane():
        stacked = jnp.stack(begun, axis=0)
        total = lax.psum_scatter(stacked, PLANE, scatter_dimension=0, tiled=True)
        return total[0].astype(WIDE)
    own, to_x, to_y = begun
    return own + to_x.astype(WIDE) + to_y.astype(WIDE)


def gather_column(shard):
    depth = lax.axis_size("grp")
    z = lax.axis_index("grp")
    if not small_plane():
        return shard
    column = jnp.zeros((depth,) + shard.shape, shard.dtype)
    held = shard
    for dz in range(depth):
        column = lax.dynamic_update_slice(column, held[None], ((z - dz) % depth, 0, 0))
        if dz + 1 < depth:
            held = shift(held, "grp", 1)
    return column


def gather_columns(column):
    if not small_plane():
        return lax.all_gather(column, ("grp",) + PLANE, axis=0, tiled=True)
    depth, rows, cols = column.shape
    y, x, c = [lax.axis_index(axis) for axis in PLANE]
    half = depth // 2
    from_x = swap(column, "sx")
    from_y = swap(column, "sy")
    corner = jnp.concatenate([swap(from_x[:half], "sy"), swap(from_y[half:], "sx")], axis=0)
    flat = jnp.zeros((depth, 2, 2, rows, cols), column.dtype)
    for dy, dx, piece in ((0, 0, column), (0, 1, from_x), (1, 0, from_y), (1, 1, corner)):
        flat = lax.dynamic_update_slice(flat, piece[:, None, None], (0, y ^ dy, x ^ dx, 0, 0))
    other = swap(flat, "sc")
    first = jnp.where(c == 0, flat, other)
    second = jnp.where(c == 0, other, flat)
    return jnp.stack([first, second], axis=3).reshape(depth * 8 * rows, cols)


def sum_begin(partial):
    if not small_plane():
        return (partial,)
    depth = lax.axis_size("grp")
    y, x, c = [lax.axis_index(axis) for axis in PLANE]
    cols = partial.shape[1]
    rows = partial.shape[0] // (depth * 8)
    value = partial.reshape(depth, 2, 2, 2, rows, cols)
    joined = pick(value, 3, c).astype(WIDE) + swap(pick(value, 3, 1 - c), "sc").astype(WIDE)
    joined = joined.astype(LOW)
    near, far = pick(joined, 1, y), pick(joined, 1, 1 - y)
    own, to_x = pick(near, 1, x), pick(near, 1, 1 - x)
    to_y, corner = pick(far, 1, x), pick(far, 1, 1 - x)
    half = depth // 2
    return own, to_x, to_y, swap(corner[:half], "sy"), swap(corner[half:], "sx")


def sum_end(begun):
    if not small_plane():
        return lax.psum_scatter(
            begun[0], ("grp",) + PLANE, scatter_dimension=0, tiled=True
        ).astype(WIDE)
    depth = lax.axis_size("grp")
    z = lax.axis_index("grp")
    own, to_x, to_y, low, high = begun
    half = depth // 2
    to_x = jnp.concatenate(
        [(to_x[:half].astype(WIDE) + low.astype(WIDE)).astype(LOW), to_x[half:]], axis=0
    )
    to_y = jnp.concatenate(
        [to_y[:half], (to_y[half:].astype(WIDE) + high.astype(WIDE)).astype(LOW)], axis=0
    )
    total = own.astype(WIDE) + swap(to_x, "sx").astype(WIDE) + swap(to_y, "sy").astype(WIDE)
    low_total = total.astype(LOW)
    result = pick(total, 0, z)
    for step in range(1, depth):
        result = result + shift(pick(low_total, 0, (z + step) % depth), "grp", step).astype(WIDE)
    return result


def scatter_all(partial):
    return sum_end(sum_begin(partial))


def rotate(values):
    half = values.shape[-1] // 2
    return jnp.concatenate([-values[:, half:], values[:, :half]], axis=-1)


def unrotate(values):
    half = values.shape[-1] // 2
    return jnp.concatenate([values[:, half:], -values[:, :half]], axis=-1)


def unit_of(raw):
    values = raw.astype(WIDE)
    inverse = lax.rsqrt(jnp.mean(values * values, axis=-1, keepdims=True) + eps_norm)
    return values * inverse, inverse


def turned(unit, gain, cos, sin):
    gained = unit * gain
    return (gained * cos + rotate(gained) * sin).astype(LOW)


def norm_back(grad_out, unit_vals, inv_rms, gain_vec):
    scaled = grad_out * gain_vec
    return inv_rms * (scaled - unit_vals * jnp.mean(scaled * unit_vals, axis=-1, keepdims=True))


NT = (((1,), (1,)), ((), ()))
TN = (((0,), (0,)), ((), ()))


def fill_bias(bias_ref, doc_q_ref, doc_k_ref):
    rows, window = bias_ref.shape
    row_at = lax.broadcasted_iota(jnp.int32, (rows, window), 0) + (window - rows)
    col_at = lax.broadcasted_iota(jnp.int32, (rows, window), 1)
    allowed = (doc_q_ref[...] == doc_k_ref[...]) & (col_at <= row_at)
    bias_ref[...] = jnp.where(allowed, 0.0, -1e30).astype(WIDE)


def attend_kernel(q_ref, kv_ref, cos_ref, sin_ref, gain_ref, doc_q_ref, doc_k_ref, o_ref, lse_ref, bias_ref):
    rows, window = bias_ref.shape

    @pl.when(pl.program_id(0) == 0)
    def _():
        fill_bias(bias_ref, doc_q_ref, doc_k_ref)

    gain_q, gain_k = gain_ref[0:1, :], gain_ref[1:2, :]
    cos_q, sin_q = cos_ref[window - rows :, :], sin_ref[window - rows :, :]
    k_unit, _ = unit_of(kv_ref[:, :HEAD_DIM])
    k_low = turned(k_unit, gain_k, cos_ref[...], sin_ref[...])
    v_low = kv_ref[:, HEAD_DIM:]
    for head in range(GROUP):
        cols = slice(head * HEAD_DIM, (head + 1) * HEAD_DIM)
        q_unit, _ = unit_of(q_ref[:, cols])
        q_low = turned(q_unit, gain_q, cos_q, sin_q) * 0.125
        scores = lax.dot_general(q_low, k_low, NT, preferred_element_type=WIDE) + bias_ref[...]
        peak = jnp.max(scores, axis=-1, keepdims=True)
        weights = jnp.exp(scores - peak)
        total = jnp.sum(weights, axis=-1, keepdims=True)
        soft_low = (weights * (1.0 / total)).astype(LOW)
        o_ref[:, cols] = jnp.dot(soft_low, v_low, preferred_element_type=WIDE).astype(LOW)
        lse_ref[0, :, head : head + 1] = peak + jnp.log(total)


def attend(q, kv, cos, sin, gain, doc_q, doc_k):
    rows, window = q.shape[0], kv.shape[0]
    fixed = lambda g: (0, 0)
    return pl.pallas_call(
        attend_kernel,
        grid=(KV_HEAD_COUNT,),
        in_specs=[
            pl.BlockSpec((rows, GROUP * HEAD_DIM), lambda g: (0, g)),
            pl.BlockSpec((window, 2 * HEAD_DIM), lambda g: (0, g)),
            pl.BlockSpec((window, HEAD_DIM), fixed),
            pl.BlockSpec((window, HEAD_DIM), fixed),
            pl.BlockSpec((2, HEAD_DIM), fixed),
            pl.BlockSpec((rows, 1), fixed),
            pl.BlockSpec((1, window), fixed),
        ],
        out_specs=[
            pl.BlockSpec((rows, GROUP * HEAD_DIM), lambda g: (0, g)),
            pl.BlockSpec((1, rows, GROUP), lambda g: (g, 0, 0)),
        ],
        out_shape=[
            jax.ShapeDtypeStruct((rows, QUERY_HEADS * HEAD_DIM), LOW),
            jax.ShapeDtypeStruct((KV_HEAD_COUNT, rows, GROUP), WIDE),
        ],
        scratch_shapes=[pltpu.VMEM((rows, window), WIDE)],
        cost_estimate=pl.CostEstimate(
            flops=4 * rows * window * HEAD_DIM * QUERY_HEADS * 4,
            transcendentals=rows * window * QUERY_HEADS,
            bytes_accessed=rows * 1280 * 4 + window * 1280,
        ),
        name="attend",
    )(q, kv, cos, sin, gain, doc_q, doc_k)


def attend_back_kernel(
    q_ref, kv_ref, cos_ref, sin_ref, gain_ref, doc_q_ref, doc_k_ref, lse_ref, dm_ref,
    dq_ref, dkv_ref, dgain_ref, bias_ref,
):
    rows, window = bias_ref.shape

    @pl.when(pl.program_id(0) == 0)
    def _():
        fill_bias(bias_ref, doc_q_ref, doc_k_ref)
        dgain_ref[...] = jnp.zeros_like(dgain_ref)

    gain_q, gain_k = gain_ref[0:1, :], gain_ref[1:2, :]
    cos_q, sin_q = cos_ref[window - rows :, :], sin_ref[window - rows :, :]
    k_unit, k_inv = unit_of(kv_ref[:, :HEAD_DIM])
    k_low = turned(k_unit, gain_k, cos_ref[...], sin_ref[...])
    v_low = kv_ref[:, HEAD_DIM:]
    dk = jnp.zeros((window, HEAD_DIM), WIDE)
    dv = jnp.zeros((window, HEAD_DIM), WIDE)
    gain_sum = jnp.zeros((1, HEAD_DIM), WIDE)
    for head in range(GROUP):
        cols = slice(head * HEAD_DIM, (head + 1) * HEAD_DIM)
        q_unit, q_inv = unit_of(q_ref[:, cols])
        q_low = turned(q_unit, gain_q, cos_q, sin_q) * 0.125
        grad = dm_ref[:, cols]
        scores = lax.dot_general(q_low, k_low, NT, preferred_element_type=WIDE) + bias_ref[...]
        soft = jnp.exp(scores - lse_ref[0, :, head : head + 1])
        d_soft = lax.dot_general(grad, v_low, NT, preferred_element_type=WIDE)
        delta = jnp.sum(soft * d_soft, axis=-1, keepdims=True)
        d_score = (soft * (d_soft - delta)).astype(LOW)
        dq_hat = jnp.dot(d_score, k_low, preferred_element_type=WIDE) * 0.125
        dk = dk + lax.dot_general(d_score, q_low, TN, preferred_element_type=WIDE)
        dv = dv + lax.dot_general(soft.astype(LOW), grad, TN, preferred_element_type=WIDE)
        dq_gained = dq_hat * cos_q + unrotate(dq_hat * sin_q)
        gain_sum = gain_sum + jnp.sum(dq_gained * q_unit, axis=0, keepdims=True)
        dq_ref[:, cols] = norm_back(dq_gained, q_unit, q_inv, gain_q).astype(LOW)
    dk_gained = dk * cos_ref[...] + unrotate(dk * sin_ref[...])
    dgain_ref[0:1, :] = dgain_ref[0:1, :] + gain_sum
    dgain_ref[1:2, :] = dgain_ref[1:2, :] + jnp.sum(dk_gained * k_unit, axis=0, keepdims=True)
    dkv_ref[:, :HEAD_DIM] = norm_back(dk_gained, k_unit, k_inv, gain_k)
    dkv_ref[:, HEAD_DIM:] = dv


def attend_back(q, kv, cos, sin, gain, doc_q, doc_k, lse, d_mix):
    rows, window = q.shape[0], kv.shape[0]
    fixed = lambda g: (0, 0)
    wide_block = pl.BlockSpec((rows, GROUP * HEAD_DIM), lambda g: (0, g))
    pair_block = pl.BlockSpec((window, 2 * HEAD_DIM), lambda g: (0, g))
    return pl.pallas_call(
        attend_back_kernel,
        grid=(KV_HEAD_COUNT,),
        in_specs=[
            wide_block,
            pair_block,
            pl.BlockSpec((window, HEAD_DIM), fixed),
            pl.BlockSpec((window, HEAD_DIM), fixed),
            pl.BlockSpec((2, HEAD_DIM), fixed),
            pl.BlockSpec((rows, 1), fixed),
            pl.BlockSpec((1, window), fixed),
            pl.BlockSpec((1, rows, GROUP), lambda g: (g, 0, 0)),
            wide_block,
        ],
        out_specs=[wide_block, pair_block, pl.BlockSpec((2, HEAD_DIM), fixed)],
        out_shape=[
            jax.ShapeDtypeStruct((rows, QUERY_HEADS * HEAD_DIM), LOW),
            jax.ShapeDtypeStruct((window, KV_HEAD_COUNT * 2 * HEAD_DIM), WIDE),
            jax.ShapeDtypeStruct((2, HEAD_DIM), WIDE),
        ],
        scratch_shapes=[pltpu.VMEM((rows, window), WIDE)],
        cost_estimate=pl.CostEstimate(
            flops=10 * rows * window * HEAD_DIM * QUERY_HEADS * 4,
            transcendentals=rows * window * QUERY_HEADS,
            bytes_accessed=rows * 1280 * 6 + window * 640 * 6,
        ),
        name="attend_back",
    )(q, kv, cos, sin, gain, doc_q, doc_k, lse, d_mix)


def feed_kernel(main, nf_ref, c_ref, wgu_ref, wd_ref, hid_ref, dgu_ref, out_ref, dnf_ref):
    width = wd_ref.shape[0]
    rest = width - main
    both = jnp.dot(nf_ref[...], wgu_ref[...], preferred_element_type=WIDE)
    d_hidden = lax.dot_general(c_ref[...], wd_ref[...], NT, preferred_element_type=WIDE)

    def one(gate, up, d_hid, hid_at, gate_at, up_at, size):
        sig = jax.nn.sigmoid(gate)
        silu = gate * sig
        hid_ref[:, hid_at : hid_at + size] = (silu * up).astype(LOW)
        dgu_ref[:, gate_at : gate_at + size] = (
            d_hid * up * (sig * (1.0 + gate * (1.0 - sig)))
        ).astype(LOW)
        dgu_ref[:, up_at : up_at + size] = (d_hid * silu).astype(LOW)

    one(both[:, :main], both[:, main : 2 * main], d_hidden[:, :main], 0, 0, main, main)
    if rest:
        one(
            both[:, 2 * main : 2 * main + rest],
            both[:, 2 * main + rest :],
            d_hidden[:, main:],
            main,
            2 * main,
            2 * main + rest,
            rest,
        )
    out_ref[...] = jnp.dot(hid_ref[...], wd_ref[...], preferred_element_type=WIDE).astype(LOW)
    dnf_ref[...] = lax.dot_general(
        dgu_ref[...], wgu_ref[...], NT, preferred_element_type=WIDE
    ).astype(LOW)


def feed(nf, c, wgu, wd, tile):
    tokens, model = nf.shape
    width = wd.shape[0]
    main = width // 128 * 128
    fixed = lambda t: (0, 0)
    by_token = lambda t: (t, 0)
    return pl.pallas_call(
        functools.partial(feed_kernel, main),
        grid=(tokens // tile,),
        in_specs=[
            pl.BlockSpec((tile, model), by_token),
            pl.BlockSpec((tile, model), by_token),
            pl.BlockSpec((model, 2 * width), fixed),
            pl.BlockSpec((width, model), fixed),
        ],
        out_specs=[
            pl.BlockSpec((tile, width), by_token),
            pl.BlockSpec((tile, 2 * width), by_token),
            pl.BlockSpec((tile, model), by_token),
            pl.BlockSpec((tile, model), by_token),
        ],
        out_shape=[
            jax.ShapeDtypeStruct((tokens, width), LOW),
            jax.ShapeDtypeStruct((tokens, 2 * width), LOW),
            jax.ShapeDtypeStruct((tokens, model), LOW),
            jax.ShapeDtypeStruct((tokens, model), LOW),
        ],
        cost_estimate=pl.CostEstimate(
            flops=2 * tokens * model * width * 6,
            transcendentals=tokens * width,
            bytes_accessed=tokens * model * 8 + model * width * 6,
        ),
        name="feed",
    )(nf, c, wgu, wd)


def row_tables(lengths, positions):
    doc_count = lengths.shape[0]
    ends_at = jnp.cumsum(lengths)
    starts_at = ends_at - lengths
    document = jnp.sum((positions[:, None] >= ends_at[None, :]).astype(jnp.int32), axis=1)
    chosen = document[:, None] == jnp.arange(doc_count, dtype=jnp.int32)[None, :]
    start_of = jnp.sum(jnp.where(chosen, starts_at[None, :], 0), axis=1)
    offsets = (positions - start_of).astype(WIDE)
    frequency = jnp.exp(
        jnp.arange(HEAD_DIM // 2, dtype=WIDE) * (-2.0 * math.log(10000.0) / HEAD_DIM)
    )
    angles = offsets[:, None] * frequency[None, :]
    cosine = jnp.cos(angles)
    sine = jnp.sin(angles)
    return (
        document,
        jnp.concatenate([cosine, cosine], axis=1),
        jnp.concatenate([sine, sine], axis=1),
    )


def adam_update(master, first_old, second_old, grad_in, clip_scale, learn_rate, decay_rate):
    clipped = grad_in * clip_scale
    first_new = beta_one * first_old + (1.0 - beta_one) * clipped
    second_new = beta_two * second_old + (1.0 - beta_two) * clipped * clipped
    first_hat = first_new / (1.0 - beta_one**step_count)
    second_hat = second_new / (1.0 - beta_two**step_count)
    master_new = master - learn_rate * (
        first_hat / (jnp.sqrt(second_hat) + adam_eps) + decay_rate * master
    )
    return (master_new, first_new, second_new)


def pair_columns(weight):
    rows = weight.shape[0]
    q_cols = QUERY_HEADS * HEAD_DIM
    pairs = weight[:, q_cols:].reshape(rows, 2, KV_HEAD_COUNT, HEAD_DIM)
    return jnp.concatenate(
        [weight[:, :q_cols], pairs.transpose(0, 2, 1, 3).reshape(rows, -1)], axis=1
    )


def unpair_columns(weight):
    rows = weight.shape[0]
    q_cols = QUERY_HEADS * HEAD_DIM
    pairs = weight[:, q_cols:].reshape(rows, KV_HEAD_COUNT, 2, HEAD_DIM)
    return jnp.concatenate(
        [weight[:, :q_cols], pairs.transpose(0, 2, 1, 3).reshape(rows, -1)], axis=1
    )


def to_slices(weight, depth, plane):
    rows, ff = weight.shape
    return (
        weight.reshape(rows, depth, plane, ff // (depth * plane))
        .transpose(2, 0, 1, 3)
        .reshape(plane, rows, ff // plane)
    )


def from_slices(slices, depth):
    plane, rows, width = slices.shape
    return (
        slices.reshape(plane, rows, depth, width // depth)
        .transpose(1, 2, 0, 3)
        .reshape(rows, plane * width)
    )


def local(
    layer_input, cotangent, doc_lengths,
    projection_weight, w_out, w_gate, w_up, w_down, norm_gains,
    first_moment_projection, m_out, m_gate, m_up, m_down, m_gains,
    second_moment_projection, v_out, v_gate, v_up, v_down, v_gains,
):
    depth = lax.axis_size("grp")
    plane = lax.axis_size("sy") * lax.axis_size("sx") * lax.axis_size("sc")
    z = lax.axis_index("grp")
    member = plane_index()
    tokens, model = layer_input.shape[1], layer_input.shape[2]
    seq_length = depth * tokens
    longest = seq_length // 2
    back_blocks = min(depth - 1, -(-(longest - 1) // tokens))
    window = (back_blocks + 1) * tokens
    q_cols = QUERY_HEADS * HEAD_DIM

    device = z * plane + member
    gain_rows = jnp.zeros((depth * plane, norm_gains.shape[0]), WIDE)
    gain_rows = lax.dynamic_update_slice(
        gain_rows, norm_gains.astype(LOW).astype(WIDE)[None], (device, 0)
    )
    gains = butterfly_sum(gain_rows).reshape(-1)
    gain_attn = gains[:model]
    gain_ffn = gains[model : 2 * model]
    gain_heads = gains[2 * model :].reshape(2, HEAD_DIM)

    qkv_weight = lax.all_gather(
        pair_columns(projection_weight.astype(LOW)), ("grp",) + PLANE, axis=0, tiled=True
    )
    width = w_down.shape[0] * depth
    main = width // 128 * 128
    out_column = gather_column(w_out.astype(LOW))
    down_weight = gather_column(w_down.astype(LOW))
    if small_plane():
        down_weight = down_weight.reshape(width, -1)
    else:
        down_weight = lax.all_gather(down_weight, "grp", axis=0, tiled=True)
    gate_cut = to_slices(w_gate.astype(LOW), depth, plane)
    up_cut = to_slices(w_up.astype(LOW), depth, plane)
    cut = jnp.concatenate(
        [gate_cut[..., :main], up_cut[..., :main], gate_cut[..., main:], up_cut[..., main:]], axis=-1
    )
    cut = plane_to_all(cut).reshape(-1, 2 * width)
    grad_out = cotangent[0]

    positions = (z - back_blocks) * tokens + jnp.arange(window, dtype=jnp.int32)
    document, cosine, sine = row_tables(doc_lengths[0], positions)
    doc_k = jnp.where(positions >= 0, document, -1)[None, :]
    doc_q = document[window - tokens :, None]
    inputs = layer_input[0].astype(WIDE)
    inv_attn = lax.rsqrt(jnp.mean(inputs * inputs, axis=-1, keepdims=True) + eps_norm)
    unit_attn = inputs * inv_attn
    normed = (unit_attn * gain_attn).astype(LOW)
    normed = after(normed, cut, out_column, down_weight)
    pair_own = jnp.dot(normed, qkv_weight[:, q_cols:], preferred_element_type=WIDE).astype(LOW)
    query = jnp.dot(normed, qkv_weight[:, :q_cols], preferred_element_type=WIDE).astype(LOW)
    pairs = [pair_own]
    onward = [(i, i + 1) for i in range(depth - 1)]
    backward = [(i + 1, i) for i in range(depth - 1)]
    for _ in range(back_blocks):
        pairs.append(lax.ppermute(pairs[-1], "grp", onward))
    both_weight = lax.all_gather(after(cut, pairs[1]), "grp", axis=0, tiled=True)
    out_weight = gather_columns(after(out_column, pairs[1]))
    grad_blocks = gather_plane(after(grad_out, pairs[1]))
    pair_all = jnp.concatenate(pairs[::-1], axis=0)
    mix, lse = attend(query, pair_all, cosine, sine, gain_heads, doc_q, doc_k)
    resid = inputs + jnp.dot(mix, out_weight, preferred_element_type=WIDE)
    inv_ffn = lax.rsqrt(jnp.mean(resid * resid, axis=-1, keepdims=True) + eps_norm)
    unit_ffn = resid * inv_ffn
    normed_ffn = (unit_ffn * gain_ffn).astype(LOW)

    nf_all = jnp.concatenate(gather_plane(normed_ffn), axis=0)
    c_all = jnp.concatenate(grad_blocks, axis=0)
    hidden, d_both, out_part, nf_part = feed(nf_all, c_all, both_weight, down_weight, tokens)
    split = lambda value: [value[i * tokens : (i + 1) * tokens] for i in range(plane)]
    norm_begun = scatter_begin(split(nf_part))
    d_norm_ffn = scatter_end(scatter_send(norm_begun))
    out_begun = scatter_begin(split(after(out_part, *norm_begun)))
    both_grad = lax.dot_general(nf_all, d_both, TN, preferred_element_type=WIDE).astype(LOW)
    down_grad = lax.dot_general(hidden, c_all, TN, preferred_element_type=WIDE).astype(LOW)

    gain_ffn_grad = jnp.sum(d_norm_ffn * unit_ffn, axis=0)
    d_resid = grad_out.astype(WIDE) + norm_back(d_norm_ffn, unit_ffn, inv_ffn, gain_ffn)
    d_attn = d_resid.astype(LOW)
    d_mix = lax.dot_general(d_attn, out_weight, NT, preferred_element_type=WIDE).astype(LOW)
    out_grad = lax.dot_general(mix, d_attn, TN, preferred_element_type=WIDE).astype(LOW)
    both_sum = lax.psum_scatter(both_grad, "grp", scatter_dimension=0, tiled=True)
    down_sum = lax.psum_scatter(
        after(down_grad, both_grad), "grp", scatter_dimension=0, tiled=True
    ).astype(WIDE)
    d_mix, out_begun, _, _, out_grad = lax.optimization_barrier(
        (d_mix, out_begun, both_grad, down_grad, out_grad)
    )
    out_begun = scatter_send(out_begun)
    out_begun_sum = sum_begin(out_grad)

    d_query, d_pairs, head_gain_grad = attend_back(
        query, pair_all, cosine, sine, gain_heads, doc_q, doc_k, lse, d_mix
    )
    d_query, d_pairs, out_begun, out_begun_sum = lax.optimization_barrier(
        (d_query, d_pairs, out_begun, out_begun_sum)
    )
    output = (resid + scatter_end(out_begun)).astype(LOW)
    out_sum = sum_end(out_begun_sum)
    moving = None
    for block in range(back_blocks):
        part = d_pairs[block * tokens : (block + 1) * tokens]
        if moving is not None:
            part = part + moving.astype(WIDE)
        moving = lax.ppermute(part.astype(LOW), "grp", backward)
    d_pair = d_pairs[window - tokens :]
    if moving is not None:
        d_pair = d_pair + moving.astype(WIDE)
    d_qkv = jnp.concatenate([d_query, d_pair.astype(LOW)], axis=1)
    query_grad = lax.dot_general(normed, d_query, TN, preferred_element_type=WIDE).astype(LOW)
    pair_grad = lax.dot_general(
        normed, d_qkv[:, q_cols:], TN, preferred_element_type=WIDE
    ).astype(LOW)
    d_normed = lax.dot_general(d_qkv, qkv_weight, NT, preferred_element_type=WIDE)
    gain_attn_grad = jnp.sum(d_normed * unit_attn, axis=0)
    input_grad = d_resid + norm_back(d_normed, unit_attn, inv_attn, gain_attn)

    slices = plane_to_all(both_sum.reshape(plane, -1, 2 * width))
    rest = width - main
    gate_slices = jnp.concatenate([slices[..., :main], slices[..., 2 * main : 2 * main + rest]], axis=-1)
    up_slices = jnp.concatenate([slices[..., main : 2 * main], slices[..., 2 * main + rest :]], axis=-1)
    gate_low, up_low = lax.optimization_barrier(
        (from_slices(gate_slices, depth), from_slices(up_slices, depth))
    )
    gate_sum, up_sum = gate_low.astype(WIDE), up_low.astype(WIDE)
    query_begun = sum_begin(query_grad)
    pair_begun = sum_begin(pair_grad)
    query_begun, pair_begun, _, _ = lax.optimization_barrier((query_begun, pair_begun, gate_low, up_low))
    qkv_sum = unpair_columns(jnp.concatenate([sum_end(query_begun), sum_end(pair_begun)], axis=1))
    shards = list(lax.optimization_barrier((qkv_sum, out_sum, gate_sum, up_sum, down_sum)))
    local_square = jnp.sum(shards[0] * shards[0])
    for shard in shards[1:]:
        local_square = local_square + jnp.sum(shard * shard)
    gain_grad = jnp.concatenate([gain_attn_grad, gain_ffn_grad, head_gain_grad.reshape(-1)])
    gain_count = gain_grad.shape[0]
    packed = jnp.concatenate([gain_grad, jnp.full((128,), local_square, WIDE)]).reshape(-1, 128)
    packed = butterfly_sum(packed).reshape(-1)
    gain_total = packed[:gain_count]
    grad_norm = jnp.sqrt(packed[gain_count] + jnp.sum(gain_total * gain_total))
    clip_scale = jnp.minimum(1.0, clip_level / (grad_norm + 1e-06))
    own_gains = norm_gains.shape[0]
    shards.append(lax.dynamic_slice(gain_total, (device * own_gains,), (own_gains,)))

    masters = (projection_weight, w_out, w_gate, w_up, w_down, norm_gains)
    firsts = (first_moment_projection, m_out, m_gate, m_up, m_down, m_gains)
    seconds = (second_moment_projection, v_out, v_gate, v_up, v_down, v_gains)
    results = [
        adam_update(w, m, v, g, clip_scale, lr, wd)
        for w, m, v, g, lr, wd in zip(masters, firsts, seconds, shards, learn_rates, decay_rates)
    ]
    return (
        output[None],
        input_grad[None],
        grad_norm,
        *[r[0] for r in results],
        *[r[1] for r in results],
        *[r[2] for r in results],
    )


def solution(mesh):
    depth, plane = mesh.shape["grp"], mesh.shape["seq"]
    side = math.isqrt(plane // 2)
    inner = Mesh(
        np.asarray(mesh.devices).reshape(depth, plane // 2 // side, side, 2),
        ("grp",) + PLANE,
    )
    rows = P(("grp",) + PLANE, None)
    vector = P(("grp",) + PLANE)
    block = P(PLANE, "grp", None)
    params = (rows,) * 5 + (vector,)
    return jax.shard_map(
        local,
        mesh=inner,
        in_specs=(block, block, P(PLANE, None)) + params * 3,
        out_specs=(block, block, P()) + params * 3,
        check_vma=False,
    )
```
